32 devices in a mesh: tm: 16 (over z, y, core), head: 2 (over x).
Axes of the slice: x: 2, y: 2, z: 4, core: 2. Of those that a mesh axis runs over, the one named last changes fastest.
Arguments:
- codes: int32 [16384, 8], P('tm'), may hold values from 0 to 1023
- tables: bfloat16 [8, 1024, 2048], P(None, None, 'head'), may hold values from -2.5 to 2.5
- conv_weight: bfloat16 [5, 2048, 2048], P(None, 'head'), may hold values from -0.0625 to 0.0625
- norm_gain: float32 [2048], replicated, may hold values from 0.1 to 1.9
- key_weight: bfloat16 [2048, 2048], P(None, 'head')
- value_weight: bfloat16 [2048, 2048], P(None, 'head'), may hold values from -0.125 to 0.125
- query_weight: bfloat16 [2048, 2048], P(None, 'head')
- latent_pos: int32 [512], replicated, may hold values from 0 to 4095, as said below
Outputs:
- attended: bfloat16 [512, 2048], P('tm', 'head')
The draws below stay inside these ranges and needn't reach their ends.
Inputs may be any that keep to these rules, and one draw needn't show every extreme that they name: `latent_pos`: strictly increasing; holds every multiple of 256 and the last row 4095.
All inputs are finite; a program needn't handle non-finite values.
Results may differ from the reference program's by a relative error of at most 0.04.
The reference program's roundings to bfloat16 on the way count: a program that leaves them out, or rounds other values in their place, can miss the bound.
Values may be sent and summed in bfloat16 or wider, within the bound.
No kernel may reach another device: no remote copies, remote signals or barrier semaphores. Data moves between devices by JAX's collectives and lax.ppermute only.
A program may use at most 128 MiB of HBM per device.

```python
import math
import jax
import jax.numpy as jnp
from jax import lax

D = 2048
HEADS = 16
HEAD_DIM = 128
CODEBOOKS = 8
VOCAB = 1024
KW = 5
STRIDE = 4
LAT_DEV = 32
FRAMES = 16384
ROWS = 4096
LATENTS = 512


def shared_matrix(key):
    return jax.random.normal(jax.random.fold_in(key, 11), (D, D), jnp.float32) / math.sqrt(D)


def draw_key_weight(key, part):
    return shared_matrix(key).astype(jnp.bfloat16)


def draw_query_weight(key, part):
    fresh = jax.random.normal(jax.random.fold_in(key, 12), (D, D), jnp.float32) / math.sqrt(D)
    return fresh.astype(jnp.bfloat16)


def draw_latent_pos(key, part):
    shard_rows = ROWS // (LATENTS // LAT_DEV)
    rows_all = jnp.arange(ROWS, dtype=jnp.int32)
    forced = jnp.logical_or(rows_all % shard_rows == 0, rows_all == ROWS - 1)
    shuffled = jax.random.permutation(jax.random.fold_in(key, 17), ROWS).astype(jnp.int32)
    priority = jnp.where(forced, rows_all - ROWS, shuffled)
    chosen = jnp.argsort(priority, stable=True)[:LATENTS].astype(jnp.int32)
    return jnp.sort(chosen).astype(jnp.int32)


def touch_ends(array, key, low, high):
    extent = array.shape
    place = [jax.random.randint(jax.random.fold_in(key, axis), (), 0, extent[axis]) for axis in range(len(extent))]
    array = array.at[tuple(place)].set(low)
    longest = extent.index(max(extent))
    place[longest] = (place[longest] + 1) % extent[longest]
    return array.at[tuple(place)].set(high)


def shard_levels(rng, extent, cuts, least, high):
    def one(axis_at, blocks):
        heights = jax.random.uniform(jax.random.fold_in(jax.random.fold_in(rng, 6), axis_at), (blocks,), jnp.float32, least / len(cuts), high / len(cuts))
        return jnp.repeat(jnp.exp(heights), extent[axis_at] // blocks).reshape((-1,) + (1,) * (len(extent) - axis_at - 1))

    loudness = one(*cuts[0])
    for cut in cuts[1:]:
        loudness = loudness * one(*cut)
    return loudness


def bell_draw(stream_key, dims, width, bound, shards=(), held_as=jnp.bfloat16):
    values = jax.random.normal(stream_key, dims, jnp.float32) * width
    if len(shards) > 0:
        values = shard_levels(stream_key, dims, shards, -0.22, 0.18) * values
    return jnp.clip(values, min=-bound, max=bound).astype(held_as)


def setup_inputs(seed: int = 0) -> dict:
    keys = jax.random.split(jax.random.key(seed), 9)
    return {
        "codes": touch_ends(jax.random.randint(keys[0], (FRAMES, CODEBOOKS), 0, VOCAB), jax.random.fold_in(keys[0], 1), 0, VOCAB - 1).astype(jnp.int32),
        "tables": bell_draw(keys[1], (CODEBOOKS, VOCAB, D), 0.35, 2.5, ((2, 2),)),
        "conv_weight": bell_draw(keys[2], (KW, D, D), (KW * D) ** -0.5, 0.0625, ((1, 2),)),
        "norm_gain": jnp.clip(1.0 + 0.18 * jax.random.normal(keys[3], (D,), jnp.float32), 0.1, 1.9),
        "key_weight": draw_key_weight(jax.random.fold_in(keys[8], 71), 0),
        "value_weight": bell_draw(keys[5], (D, D), D ** -0.5, 0.125, ((1, 2),)),
        "query_weight": draw_query_weight(jax.random.fold_in(keys[8], 71), 0),
        "latent_pos": draw_latent_pos(jax.random.fold_in(keys[8], 71), 0),
    }


def reference(codes, tables, conv_weight, norm_gain, key_weight, value_weight, query_weight, latent_pos):
    summed = jnp.zeros((FRAMES, D), jnp.float32)
    for codebook in range(CODEBOOKS):
        summed = summed + jnp.take(tables[codebook], codes[:, codebook], axis=0).astype(jnp.float32)
    frames = summed.astype(jnp.bfloat16)
    lag_rows = KW - STRIDE
    padded = jnp.concatenate([jnp.zeros((lag_rows, D), jnp.bfloat16), frames], 0)
    earlier = padded[:FRAMES].reshape(ROWS, STRIDE, D)[:, :lag_rows].reshape(ROWS, lag_rows * D)
    latter = frames.reshape(ROWS, STRIDE * D)
    window = jnp.concatenate([earlier, latter], 1)
    conv_out = jnp.dot(window, conv_weight.reshape(KW * D, D), preferred_element_type=jnp.float32).astype(jnp.bfloat16)
    widened = conv_out.astype(jnp.float32)
    inverse = lax.rsqrt(lax.optimization_barrier(jnp.sum(widened * widened, 1)) / D + 1e-06)
    scaled = (widened * norm_gain.astype(jnp.float32)[None, :]).astype(jnp.bfloat16)
    key_rows = (inverse[:, None] * jnp.dot(scaled, key_weight, preferred_element_type=jnp.float32)).astype(jnp.bfloat16)
    value_rows = (inverse[:, None] * jnp.dot(scaled, value_weight, preferred_element_type=jnp.float32)).astype(jnp.bfloat16)
    picked = jnp.take(scaled, latent_pos, axis=0)
    picked_inverse = jnp.take(inverse, latent_pos, axis=0)
    queries = (picked_inverse[:, None] * jnp.dot(picked, query_weight, preferred_element_type=jnp.float32)).astype(jnp.bfloat16)
    query_heads = queries.reshape(LATENTS, HEADS, HEAD_DIM).transpose(1, 0, 2)
    key_heads = key_rows.reshape(ROWS, HEADS, HEAD_DIM).transpose(1, 0, 2)
    value_heads = value_rows.reshape(ROWS, HEADS, HEAD_DIM).transpose(1, 0, 2)
    visible = jnp.arange(ROWS, dtype=jnp.int32)[None, :] <= latent_pos[:, None]

    def one_head(operands):
        query_head, key_head, value_head = operands
        scores = jnp.dot(query_head, key_head.T, preferred_element_type=jnp.float32) * (1.0 / math.sqrt(HEAD_DIM))
        scores = jnp.where(visible, scores, -1e+30)
        largest = lax.optimization_barrier(jnp.max(scores, 1, keepdims=True))
        weights = jnp.exp(scores - largest) * visible.astype(jnp.float32)
        row_sums = lax.optimization_barrier(jnp.sum(weights, 1, keepdims=True))
        product = jnp.dot(weights.astype(jnp.bfloat16), value_head, preferred_element_type=jnp.float32)
        return product / row_sums
    result = lax.map(one_head, (query_heads, key_heads, value_heads))
    return result.transpose(1, 0, 2).reshape(LATENTS, D).astype(jnp.bfloat16)
```

```python
import functools
import math

import jax
import jax.numpy as jnp
from jax import lax
from jax.experimental import pallas as pl
from jax.experimental.pallas import tpu as pltpu
from jax.sharding import PartitionSpec as P

HEAD_DIM = 128
STRIDE = 4
PAD = 16
LANES = 128
VMEM = pltpu.VMEM
HIDDEN = -1e30


def exchange_stages(count):
    stages, remaining = [], count
    while remaining > 2:
        factor = 4 if remaining % 4 == 0 and remaining // 4 >= 2 else 2
        step = remaining // factor
        stages.append([step * k for k in range(1, factor)])
        remaining = step
    return stages


def swapped(value, axis, offset):
    count = lax.axis_size(axis)
    return lax.ppermute(value, axis, [(i, i ^ offset) for i in range(count)])


def gathered(value, axis, stages):
    offsets = [0]
    for stage in stages:
        value = jnp.concatenate([value] + [swapped(value, axis, d) for d in stage], 0)
        offsets = [o ^ d for d in [0] + stage for o in offsets]
    return value, offsets


def row_tiles(rows):
    parts = max(1, round(rows / 208))
    unit = PAD * parts
    padded = -(-rows // unit) * unit
    return padded, padded // parts


def embed_conv(codes, tables, conv_weight, rows, extra, tile, first):
    total = codes.shape[0]
    books, vocab, width = tables.shape
    taps, _, features = conv_weight.shape
    span = rows + extra
    block = min(512, features)

    def body(codes_ref, tables_in, conv_in, part_ref, *rest):
        if first:
            tables_ref, conv_ref, frames_ref, lag_ref, table_sem, conv_sem = rest
            table_copies = [
                pltpu.make_async_copy(tables_in.at[c], tables_ref.at[c], table_sem.at[c])
                for c in range(books)
            ]
            conv_copies = [
                pltpu.make_async_copy(conv_in.at[k], conv_ref.at[k], conv_sem.at[k])
                for k in range(taps)
            ]
            for copy in table_copies:
                copy.start()
        else:
            tables_ref, conv_ref = tables_in, conv_in
            frames_ref, lag_ref = rest

        def one_tile(r, arrive):
            found = None
            for c in range(books):
                if arrive:
                    table_copies[c].wait()
                    if c < taps:
                        conv_copies[c].start()
                hot = codes_ref[r, c : c + 1] == lax.broadcasted_iota(jnp.int32, (tile, vocab), 1)
                got = jnp.dot(
                    hot.astype(jnp.float32).astype(jnp.bfloat16),
                    tables_ref[c],
                    preferred_element_type=jnp.float32,
                )
                found = got if found is None else found + got
            frames_ref[r, :] = found.astype(jnp.bfloat16)

        begin = 0
        if first:
            one_tile(pl.ds(0, tile), True)
            begin = 1
        if total // tile > begin:

            def step(t, carry):
                one_tile(pl.ds(pl.multiple_of(t * tile, tile), tile), False)
                return carry

            lax.fori_loop(begin, total // tile, step, 0)

        last = frames_ref[pl.ds((STRIDE - 1) * span, rows), :].astype(jnp.float32)
        before = frames_ref[pl.ds(STRIDE * span, PAD), :].astype(jnp.float32)[0:1]
        moved = pltpu.roll(last, 1, 0)
        line = lax.broadcasted_iota(jnp.int32, (rows, width), 0)
        lag_ref[pl.ds(0, rows), :] = jnp.where(line == 0, before, moved).astype(jnp.bfloat16)
        if extra:
            lag_ref[pl.ds(rows, extra), :] = frames_ref[pl.ds(STRIDE * span + PAD, extra), :]
        if first:
            for copy in conv_copies:
                copy.wait()
        for column in range(0, features, block):
            found = jnp.dot(
                lag_ref[...],
                conv_ref[0, :, column : column + block],
                preferred_element_type=jnp.float32,
            )
            for k in range(1, taps):
                found += jnp.dot(
                    frames_ref[pl.ds((k - 1) * span, span), :],
                    conv_ref[k, :, column : column + block],
                    preferred_element_type=jnp.float32,
                )
            part_ref[:, column : column + block] = found.astype(jnp.bfloat16)

    vmem = pl.BlockSpec(memory_space=VMEM)
    held = pl.BlockSpec(memory_space=pl.ANY) if first else vmem
    part = jax.ShapeDtypeStruct((span, features), jnp.bfloat16)
    scratch = [VMEM((total, width), jnp.bfloat16), VMEM((span, width), jnp.bfloat16)]
    if first:
        scratch += [pltpu.SemaphoreType.DMA((books,)), pltpu.SemaphoreType.DMA((taps,))]
    return pl.pallas_call(
        body,
        in_specs=[vmem, held, held],
        out_specs=[vmem] * 3 if first else vmem,
        out_shape=[
            part,
            VMEM(tables.shape, tables.dtype),
            VMEM(conv_weight.shape, conv_weight.dtype),
        ]
        if first
        else part,
        scratch_shapes=scratch,
        compiler_params=pltpu.CompilerParams(vmem_limit_bytes=16 << 20),
        cost_estimate=pl.CostEstimate(
            flops=2 * total * books * vocab * width + 2 * span * taps * width * features,
            bytes_accessed=36 << 20 if first else 4 << 20,
            transcendentals=0,
        ),
        name="embed_conv",
    )(codes, tables, conv_weight)


def summed_rows(part_refs, gain_ref, where):
    total = part_refs[0][where, :].astype(jnp.float32)
    for ref in part_refs[1:]:
        total = total + ref[where, :].astype(jnp.float32)
    conv_out = total.astype(jnp.bfloat16).astype(jnp.float32)
    mean = jnp.sum(conv_out * conv_out, 1, keepdims=True) / conv_out.shape[1]
    inverse = lax.rsqrt(mean + 1e-06)
    return (conv_out * gain_ref[...]).astype(jnp.bfloat16), inverse


def project(parts, gain, weights, begin, rows, name):
    features, columns = weights[0].shape
    count = len(parts)
    block = min(512, columns)

    def body(*refs):
        part_refs, gain_ref = refs[:count], refs[count]
        weight_refs = refs[count + 1 : count + 1 + len(weights)]
        out_ref = refs[count + 1 + len(weights)]
        scaled, inverse = summed_rows(part_refs, gain_ref, pl.ds(begin, rows))
        for i, weight_ref in enumerate(weight_refs):
            for column in range(0, columns, block):
                found = jnp.dot(
                    scaled,
                    weight_ref[:, column : column + block],
                    preferred_element_type=jnp.float32,
                )
                at = i * columns + column
                out_ref[:, at : at + block] = (inverse * found).astype(jnp.bfloat16)

    vmem = pl.BlockSpec(memory_space=VMEM)
    return pl.pallas_call(
        body,
        in_specs=[vmem] * (count + 1 + len(weights)),
        out_specs=vmem,
        out_shape=jax.ShapeDtypeStruct((rows, columns * len(weights)), jnp.bfloat16),
        compiler_params=pltpu.CompilerParams(vmem_limit_bytes=16 << 20),
        cost_estimate=pl.CostEstimate(
            flops=2 * rows * features * columns * len(weights),
            bytes_accessed=2 * features * columns * len(weights),
            transcendentals=0,
        ),
        name=name,
    )(*parts, gain, *weights)


def attend(place, slots, queries, keys_values, latent_rows):
    latents, width = queries.shape
    owners = slots.shape[0]
    each = latents // owners
    heads = width // HEAD_DIM
    rows = [kv.shape[0] for kv in keys_values]
    all_rows = sum(rows)

    def body(place_ref, slots_ref, q_ref, pos_ref, *rest):
        kv_refs = rest[: len(rows)]
        out_ref, query_ref = rest[len(rows) :]
        for owner in range(owners):
            at = pl.multiple_of(slots_ref[owner] * each, each)
            query_ref[pl.ds(owner * each, each), :] = q_ref[pl.ds(at, each), :]
        lane = lax.broadcasted_iota(jnp.int32, (latents, LANES), 1)
        stats = jnp.zeros((latents, LANES), jnp.float32)
        line = lax.broadcasted_iota(jnp.int32, (latents, all_rows), 1)
        base, start = jnp.zeros((latents, all_rows), jnp.int32), 0
        for i, count in enumerate(rows):
            base = jnp.where(line >= start, place_ref[i] - start, base)
            start += count
        visible = (line + base) <= pos_ref[...]
        for head in range(heads):
            here = slice(head * HEAD_DIM, (head + 1) * HEAD_DIM)
            there = slice(width + head * HEAD_DIM, width + (head + 1) * HEAD_DIM)
            keys = jnp.concatenate([ref[:, here] for ref in kv_refs], 0)
            values = jnp.concatenate([ref[:, there] for ref in kv_refs], 0)
            scores = lax.dot_general(
                query_ref[:, here],
                keys,
                (((1,), (1,)), ((), ())),
                preferred_element_type=jnp.float32,
            ) * (1.0 / math.sqrt(HEAD_DIM))
            scores = jnp.where(visible, scores, HIDDEN)
            largest = jnp.max(scores, 1, keepdims=True)
            weights = jnp.where(visible, jnp.exp(scores - largest), 0.0)
            total = jnp.sum(weights, 1, keepdims=True)
            product = jnp.dot(
                weights.astype(jnp.bfloat16), values, preferred_element_type=jnp.float32
            )
            out_ref[:, here] = product.astype(jnp.bfloat16)
            for i, value in enumerate((largest, total)):
                for piece in range(3):
                    part = value.astype(jnp.bfloat16).astype(jnp.float32)
                    stats = jnp.where(lane == (3 * i + piece) * heads + head, part, stats)
                    value = value - part
        out_ref[:, width : width + LANES] = stats.astype(jnp.bfloat16)

    vmem = pl.BlockSpec(memory_space=VMEM)
    smem = pl.BlockSpec(memory_space=pltpu.SMEM)
    return pl.pallas_call(
        body,
        in_specs=[smem, smem] + [vmem] * (2 + len(rows)),
        out_specs=vmem,
        out_shape=jax.ShapeDtypeStruct((latents, width + LANES), jnp.bfloat16),
        scratch_shapes=[VMEM((latents, width), jnp.bfloat16)],
        compiler_params=pltpu.CompilerParams(vmem_limit_bytes=24 << 20),
        cost_estimate=pl.CostEstimate(
            flops=4 * latents * all_rows * width,
            bytes_accessed=4 << 20,
            transcendentals=latents * all_rows * heads,
        ),
        name="attend",
    )(place, slots, queries, latent_rows, *keys_values)


def merge(partials, owners):
    each = partials.shape[0] // owners
    width = partials.shape[1] - LANES
    heads = width // HEAD_DIM

    def body(in_ref, out_ref):
        largest, total = [], []
        for owner in range(owners):
            stats = in_ref[pl.ds(owner * each, each), width:].astype(jnp.float32)
            column = lambda i: stats[:, i * heads : (i + 1) * heads]
            largest.append(column(0) + column(1) + column(2))
            total.append(column(3) + column(4) + column(5))
        top = functools.reduce(jnp.maximum, largest)
        factors = [jnp.exp(value - top) for value in largest]
        bottom = sum(f * t for f, t in zip(factors, total))
        for head in range(heads):
            here = slice(head * HEAD_DIM, (head + 1) * HEAD_DIM)
            found = jnp.zeros((each, HEAD_DIM), jnp.float32)
            for owner in range(owners):
                value = in_ref[pl.ds(owner * each, each), here].astype(jnp.float32)
                found += factors[owner][:, head : head + 1] * value
            out_ref[:, here] = (found / bottom[:, head : head + 1]).astype(jnp.bfloat16)

    vmem = pl.BlockSpec(memory_space=VMEM)
    return pl.pallas_call(
        body,
        in_specs=[vmem],
        out_specs=vmem,
        out_shape=jax.ShapeDtypeStruct((each, width), jnp.bfloat16),
        name="merge",
    )(partials)


def on_device(
    codes, tables, conv_weight, norm_gain, key_weight, value_weight, query_weight, latent_pos
):
    shards = lax.axis_size("tm")
    heads_axis = lax.axis_size("head")
    me = lax.axis_index("tm")
    frame_count, books = codes.shape
    taps = conv_weight.shape[0]
    lag = taps - STRIDE
    row_count = frame_count // STRIDE
    mine = latent_pos.shape[0] // shards
    stages = exchange_stages(shards)

    all_codes, offsets = gathered(codes.astype(jnp.int16), "tm", stages + [[1]])
    place_of = jnp.asarray([offsets.index(i) for i in range(shards)], jnp.int32)
    my_rows = lax.dynamic_slice(latent_pos, (me * mine,), (mine,))
    wanted = STRIDE * my_rows[None, :] - lag + jnp.arange(taps, dtype=jnp.int32)[:, None]
    wanted = jnp.concatenate([wanted.reshape(-1), (me * frame_count - 1)[None]])
    safe = jnp.maximum(wanted, 0)
    line = place_of[(safe // frame_count) ^ me] * frame_count + safe % frame_count
    fetched = jnp.take(all_codes, line, axis=0).astype(jnp.int32)
    fetched = jnp.where(wanted[:, None] >= 0, fetched, -1)
    window_codes = fetched[: taps * mine].reshape(taps, mine, books)
    phases = codes.reshape(row_count, STRIDE, books).transpose(1, 0, 2)

    gain = norm_gain[None, :]
    cuts = [(0, row_count // 4, mine), (row_count // 4, row_count * 3 // 8, 0)]
    cuts += [(row_count * 5 // 8, row_count * 3 // 8, 0)]
    held = (tables, conv_weight)
    partner_parts = []
    chunks = []
    queries = None
    for index, (begin, rows, extra) in enumerate(cuts):
        pieces = []
        for phase in range(STRIDE):
            pieces.append(phases[phase, begin : begin + rows])
            if extra:
                pieces.append(window_codes[lag + phase])
        before = fetched[taps * mine :] if begin == 0 else phases[STRIDE - 1, begin - 1 : begin]
        pieces += [before, jnp.full((PAD - 1, books), -1, jnp.int32)]
        if extra:
            pieces.append(window_codes[0])
        used = STRIDE * (rows + extra) + PAD + extra
        padded, tile = row_tiles(used)
        if padded > used:
            pieces.append(jnp.full((padded - used, books), -1, jnp.int32))
        chunk_codes = jnp.concatenate(pieces, 0)
        made = embed_conv(chunk_codes, *held, rows, extra, tile, index == 0)
        if index == 0:
            part, *held = made
        else:
            part = made
        if extra:
            window_parts = [part[rows:]]
            window_parts += [swapped(part[rows:], "head", d) for d in range(1, heads_axis)]
            queries = project(window_parts, gain, [query_weight], 0, extra, "queries")
            part = part[:rows]
        parts = [part] + [swapped(part, "head", d) for d in range(1, heads_axis)]
        chunks.append(project(parts, gain, [key_weight, value_weight], 0, rows, "keys_values"))
    all_queries, offsets = gathered(queries, "tm", stages)
    others = [swapped(chunk, "tm", 1) for chunk in chunks]

    owners = shards // 2
    slot_of = jnp.asarray([offsets.index(2 * i) for i in range(owners)], jnp.int32)
    slots = slot_of[jnp.arange(owners, dtype=jnp.int32) ^ (me // 2)]
    place = jnp.stack(
        [me * row_count + cut[0] for cut in cuts] + [(me ^ 1) * row_count + cut[0] for cut in cuts]
    ).astype(jnp.int32)
    by_core = latent_pos.reshape(owners, 2, mine)
    latent_rows = lax.dynamic_index_in_dim(by_core, me % 2, 1, False).reshape(owners * mine, 1)
    partials = attend(place, slots, all_queries, chunks + others, latent_rows)
    groups = [[2 * i + core for i in range(owners)] for core in range(2)]
    partials = lax.all_to_all(
        partials, "tm", 0, 0, axis_index_groups=groups, tiled=True
    )
    return merge(partials, owners)


def solution(mesh):
    placed = (
        P("tm", None),
        P(None, None, "head"),
        P(None, "head", None),
        P(),
        P(None, "head"),
        P(None, "head"),
        P(None, "head"),
        P(),
    )
    return jax.shard_map(
        on_device, mesh=mesh, in_specs=placed, out_specs=P("tm", "head"), check_vma=False
    )
```

```python
import functools
import math

import jax
import jax.numpy as jnp
from jax import lax
from jax.experimental import pallas as pl
from jax.experimental.pallas import tpu as pltpu
from jax.sharding import PartitionSpec as P

HEAD_DIM = 128
STRIDE = 4
PAD = 16
LANES = 128
VMEM = pltpu.VMEM
HIDDEN = -1e30
EMBED_LIMIT = 4 << 20
PROJECT_LIMIT = 8 << 20


def exchange_stages(count):
    stages, remaining = [], count
    while remaining > 2:
        factor = 4 if remaining % 4 == 0 and remaining // 4 >= 2 else 2
        step = remaining // factor
        stages.append([step * k for k in range(1, factor)])
        remaining = step
    return stages


def swapped(value, axis, offset):
    count = lax.axis_size(axis)
    return lax.ppermute(value, axis, [(i, i ^ offset) for i in range(count)])


def gathered(value, axis, stages):
    offsets, pieces = [0], [value]
    for stage in stages:
        whole = jnp.concatenate(pieces, 0)
        pieces = pieces + [swapped(whole, axis, d) for d in stage]
        offsets = [o ^ d for d in [0] + stage for o in offsets]
    return pieces, offsets


def row_tiles(rows):
    parts = max(1, round(rows / 208))
    unit = PAD * parts
    padded = -(-rows // unit) * unit
    return padded, padded // parts


def embed_conv(phases, table_source, conv_source, cut, windows, first, keep):
    begin, rows = cut
    books, vocab, width = table_source.shape
    taps, _, features = conv_source.shape
    extra = 0 if windows is None else (windows[1].shape[0] - PAD) // taps
    span = rows + extra
    total, tile = row_tiles((STRIDE * span) + PAD + extra)
    block = min(512, features)

    def body(*refs):
        phases_ref, refs = refs[0], refs[1:]
        if extra:
            (all_ref, line_ref), refs = refs[:2], refs[2:]
        tables_in, conv_in, part_ref, *refs = refs
        if first:
            *refs, table_sem, conv_sem = refs
            if keep:
                tables_ref, conv_ref, *refs = refs
            else:
                *refs, tables_ref, conv_ref = refs
            table_copies = [
                pltpu.make_async_copy(tables_in.at[c], tables_ref.at[c], table_sem.at[c])
                for c in range(books)
            ]
            conv_copies = [
                pltpu.make_async_copy(conv_in.at[k], conv_ref.at[k], conv_sem.at[k])
                for k in range(taps)
            ]
            for copy in table_copies:
                copy.start()
        else:
            tables_ref, conv_ref = tables_in, conv_in
        codes_ref, frames_ref, lag_ref = refs

        for phase in range(STRIDE):
            codes_ref[pl.ds(phase * span, rows), :] = phases_ref[phase, pl.ds(begin, rows), :]
        tail = STRIDE * span
        if extra:
            line = line_ref[...]
            count = line.shape[0]
            groups, lanes = all_ref.shape[0], all_ref.shape[1] // books
            wide = all_ref[...].astype(jnp.int32)
            pick = (line // lanes == lax.broadcasted_iota(jnp.int32, (count, groups), 1)).astype(
                jnp.float32
            ).astype(jnp.bfloat16)
            low = (wide % 32).astype(jnp.float32).astype(jnp.bfloat16)
            high = (wide // 32).astype(jnp.float32).astype(jnp.bfloat16)
            found = jnp.dot(pick, high, preferred_element_type=jnp.float32) * 32.0 + jnp.dot(
                pick, low, preferred_element_type=jnp.float32
            )
            lane = lax.broadcasted_iota(jnp.int32, (count, lanes), 1)
            fetched = jnp.zeros((count, books), jnp.int32)
            column = lax.broadcasted_iota(jnp.int32, (count, books), 1)
            for c in range(books):
                one = jnp.where(lane == line % lanes, found[:, c * lanes : (c + 1) * lanes], 0.0)
                one = jnp.sum(one, 1, keepdims=True).astype(jnp.int32)
                fetched = jnp.where(column == c, one, fetched)
            fetched = jnp.where(line >= 0, fetched, -1)
            codes_ref[pl.ds(tail, PAD + extra), :] = fetched[: PAD + extra]
            for k in range(1, taps):
                codes_ref[pl.ds((k - 1) * span + rows, extra), :] = fetched[
                    PAD + k * extra : PAD + (k + 1) * extra
                ]
        else:
            codes_ref[pl.ds(tail, PAD), :] = phases_ref[STRIDE - 1, pl.ds(begin - PAD, PAD), :]
        used = tail + PAD + extra
        if total > used:
            codes_ref[pl.ds(used, total - used), :] = jnp.full((total - used, books), -1, jnp.int32)

        def one_tile(r, arrive):
            found = None
            for c in range(books):
                if arrive:
                    table_copies[c].wait()
                    if c < taps:
                        conv_copies[c].start()
                hot = codes_ref[r, c : c + 1] == lax.broadcasted_iota(jnp.int32, (tile, vocab), 1)
                got = jnp.dot(
                    hot.astype(jnp.float32).astype(jnp.bfloat16),
                    tables_ref[c],
                    preferred_element_type=jnp.float32,
                )
                found = got if found is None else found + got
            frames_ref[r, :] = found.astype(jnp.bfloat16)

        ready = 0
        if first:
            one_tile(pl.ds(0, tile), True)
            ready = 1
        if total // tile > ready:

            def step(t, carry):
                one_tile(pl.ds(pl.multiple_of(t * tile, tile), tile), False)
                return carry

            lax.fori_loop(ready, total // tile, step, 0)

        last = frames_ref[pl.ds((STRIDE - 1) * span, rows), :].astype(jnp.float32)
        before = frames_ref[pl.ds(tail, PAD), :].astype(jnp.float32)[PAD - 1 :]
        moved = pltpu.roll(last, 1, 0)
        line = lax.broadcasted_iota(jnp.int32, (rows, width), 0)
        lag_ref[pl.ds(0, rows), :] = jnp.where(line == 0, before, moved).astype(jnp.bfloat16)
        if extra:
            lag_ref[pl.ds(rows, extra), :] = frames_ref[pl.ds(tail + PAD, extra), :]
        if first:
            for copy in conv_copies:
                copy.wait()
        for column in range(0, features, block):
            found = jnp.dot(
                lag_ref[...],
                conv_ref[0, :, column : column + block],
                preferred_element_type=jnp.float32,
            )
            for k in range(1, taps):
                found += jnp.dot(
                    frames_ref[pl.ds((k - 1) * span, span), :],
                    conv_ref[k, :, column : column + block],
                    preferred_element_type=jnp.float32,
                )
            part_ref[:, column : column + block] = found.astype(jnp.bfloat16)

    vmem = pl.BlockSpec(memory_space=VMEM)
    held = pl.BlockSpec(memory_space=pl.ANY) if first else vmem
    part = jax.ShapeDtypeStruct((span, features), jnp.bfloat16)
    scratch = [
        VMEM((total, books), jnp.int32),
        VMEM((total, width), jnp.bfloat16),
        VMEM((span, width), jnp.bfloat16),
    ]
    big = [VMEM(held.shape, held.dtype) for held in (table_source, conv_source)]
    limit = EMBED_LIMIT
    if first:
        if not keep:
            scratch += big
            limit += 2 * (table_source.size + conv_source.size)
        scratch += [pltpu.SemaphoreType.DMA((books,)), pltpu.SemaphoreType.DMA((taps,))]
    operands = [phases] + list(windows or ())
    return pl.pallas_call(
        body,
        in_specs=[vmem] * len(operands) + [held, held],
        out_specs=[vmem] * 3 if keep else [vmem],
        out_shape=[part] + big if keep else [part],
        scratch_shapes=scratch,
        compiler_params=pltpu.CompilerParams(vmem_limit_bytes=limit),
        cost_estimate=pl.CostEstimate(
            flops=2 * total * books * vocab * width + 2 * span * taps * width * features,
            bytes_accessed=36 << 20 if first else 4 << 20,
            transcendentals=0,
        ),
        name="embed_conv",
    )(*operands, table_source, conv_source)


def summed_rows(part_refs, gain_ref, where):
    total = part_refs[0][where, :].astype(jnp.float32)
    for ref in part_refs[1:]:
        total = total + ref[where, :].astype(jnp.float32)
    conv_out = total.astype(jnp.bfloat16).astype(jnp.float32)
    mean = jnp.sum(conv_out * conv_out, 1, keepdims=True) / conv_out.shape[1]
    inverse = lax.rsqrt(mean + 1e-06)
    return (conv_out * gain_ref[...]).astype(jnp.bfloat16), inverse


def project(groups, gain, weights, name):
    features, columns = weights[0].shape
    block = min(512, columns)
    operands = [part for group in groups for part in group[0]]
    rows = sum(group[2] for group in groups)
    count = len(operands)

    def body(*refs):
        part_refs, gain_ref = refs[:count], refs[count]
        weight_refs = refs[count + 1 : count + 1 + len(weights)]
        out_ref = refs[count + 1 + len(weights)]
        pieces, at = [], 0
        for parts, begin, size in groups:
            pieces.append(summed_rows(part_refs[at : at + len(parts)], gain_ref, pl.ds(begin, size)))
            at += len(parts)
        scaled = jnp.concatenate([piece[0] for piece in pieces], 0)
        inverse = jnp.concatenate([piece[1] for piece in pieces], 0)
        for i, weight_ref in enumerate(weight_refs):
            for column in range(0, columns, block):
                found = jnp.dot(
                    scaled,
                    weight_ref[:, column : column + block],
                    preferred_element_type=jnp.float32,
                )
                at = i * columns + column
                out_ref[:, at : at + block] = (inverse * found).astype(jnp.bfloat16)

    vmem = pl.BlockSpec(memory_space=VMEM)
    return pl.pallas_call(
        body,
        in_specs=[vmem] * (count + 1 + len(weights)),
        out_specs=vmem,
        out_shape=jax.ShapeDtypeStruct((rows, columns * len(weights)), jnp.bfloat16),
        compiler_params=pltpu.CompilerParams(vmem_limit_bytes=PROJECT_LIMIT),
        cost_estimate=pl.CostEstimate(
            flops=2 * rows * features * columns * len(weights),
            bytes_accessed=2 * features * columns * len(weights),
            transcendentals=0,
        ),
        name=name,
    )(*operands, gain, *weights)


def attend(place, owner_of, queries, keys_values, runs, latent_rows):
    width = queries[0].shape[1]
    owners = owner_of.shape[0]
    latents = latent_rows.shape[0]
    each = latents // owners
    heads = width // HEAD_DIM
    all_rows = sum(runs)
    pieces = len(queries)

    def body(place_ref, owner_ref, pos_ref, *rest):
        q_refs, kv_refs = rest[:pieces], rest[pieces:-2]
        out_ref, query_ref = rest[-2:]
        block = 0
        for q_ref in q_refs:
            for i in range(q_ref.shape[0] // each):
                at = pl.multiple_of(owner_ref[block] * each, each)
                query_ref[pl.ds(at, each), :] = q_ref[pl.ds(i * each, each), :]
                block += 1
        lane = lax.broadcasted_iota(jnp.int32, (latents, LANES), 1)
        stats = jnp.zeros((latents, LANES), jnp.float32)
        line = lax.broadcasted_iota(jnp.int32, (1, all_rows), 1)
        base, start = jnp.zeros((1, all_rows), jnp.int32), 0
        for i, count in enumerate(runs):
            base = jnp.where(line >= start, place_ref[i] - start, base)
            start += count
        visible = (line + base) <= pos_ref[...]
        for head in range(heads):
            here = slice(head * HEAD_DIM, (head + 1) * HEAD_DIM)
            there = slice(width + head * HEAD_DIM, width + (head + 1) * HEAD_DIM)
            keys = jnp.concatenate([ref[:, here] for ref in kv_refs], 0)
            values = jnp.concatenate([ref[:, there] for ref in kv_refs], 0)
            scores = lax.dot_general(
                query_ref[:, here],
                keys,
                (((1,), (1,)), ((), ())),
                preferred_element_type=jnp.float32,
            ) * (1.0 / math.sqrt(HEAD_DIM))
            scores = jnp.where(visible, scores, HIDDEN)
            largest = jnp.max(scores, 1, keepdims=True)
            weights = jnp.where(visible, jnp.exp(scores - largest), 0.0)
            total = jnp.sum(weights, 1, keepdims=True)
            product = jnp.dot(
                weights.astype(jnp.bfloat16), values, preferred_element_type=jnp.float32
            )
            out_ref[:, here] = product.astype(jnp.bfloat16)
            for i, value in enumerate((largest, total)):
                for piece in range(3):
                    part = value.astype(jnp.bfloat16).astype(jnp.float32)
                    stats = jnp.where(lane == (3 * i + piece) * heads + head, part, stats)
                    value = value - part
        out_ref[:, width : width + LANES] = stats.astype(jnp.bfloat16)

    vmem = pl.BlockSpec(memory_space=VMEM)
    smem = pl.BlockSpec(memory_space=pltpu.SMEM)
    return pl.pallas_call(
        body,
        in_specs=[smem, smem] + [vmem] * (1 + pieces + len(keys_values)),
        out_specs=vmem,
        out_shape=jax.ShapeDtypeStruct((latents, width + LANES), jnp.bfloat16),
        scratch_shapes=[VMEM((latents, width), jnp.bfloat16)],
        compiler_params=pltpu.CompilerParams(vmem_limit_bytes=24 << 20),
        cost_estimate=pl.CostEstimate(
            flops=4 * latents * all_rows * width,
            bytes_accessed=4 << 20,
            transcendentals=latents * all_rows * heads,
        ),
        name="attend",
    )(place, owner_of, latent_rows, *queries, *keys_values)


def merge(partials, owners):
    each = partials.shape[0] // owners
    width = partials.shape[1] - LANES
    heads = width // HEAD_DIM

    def body(in_ref, out_ref):
        largest, total = [], []
        for owner in range(owners):
            stats = in_ref[pl.ds(owner * each, each), width:].astype(jnp.float32)
            column = lambda i: stats[:, i * heads : (i + 1) * heads]
            largest.append(column(0) + column(1) + column(2))
            total.append(column(3) + column(4) + column(5))
        top = functools.reduce(jnp.maximum, largest)
        factors = [jnp.exp(value - top) for value in largest]
        bottom = sum(f * t for f, t in zip(factors, total))
        for head in range(heads):
            here = slice(head * HEAD_DIM, (head + 1) * HEAD_DIM)
            found = jnp.zeros((each, HEAD_DIM), jnp.float32)
            for owner in range(owners):
                value = in_ref[pl.ds(owner * each, each), here].astype(jnp.float32)
                found += factors[owner][:, head : head + 1] * value
            out_ref[:, here] = (found / bottom[:, head : head + 1]).astype(jnp.bfloat16)

    vmem = pl.BlockSpec(memory_space=VMEM)
    return pl.pallas_call(
        body,
        in_specs=[vmem],
        out_specs=vmem,
        out_shape=jax.ShapeDtypeStruct((each, width), jnp.bfloat16),
        name="merge",
    )(partials)


def on_device(
    codes, tables, conv_weight, norm_gain, key_weight, value_weight, query_weight, latent_pos
):
    shards = lax.axis_size("tm")
    heads_axis = lax.axis_size("head")
    me = lax.axis_index("tm")
    frame_count, books = codes.shape
    taps = conv_weight.shape[0]
    lag = taps - STRIDE
    row_count = frame_count // STRIDE
    mine = latent_pos.shape[0] // shards
    stages = exchange_stages(shards)

    lines = codes.astype(jnp.int16).reshape(frame_count // LANES, LANES, books)
    lines = lines.transpose(0, 2, 1).reshape(frame_count // LANES, books * LANES)
    pieces, offsets = gathered(lines, "tm", stages + [[1]])
    all_lines = jnp.concatenate(pieces, 0)
    my_rows = lax.dynamic_slice(latent_pos, (me * mine,), (mine,))
    wanted = STRIDE * my_rows[None, :] - lag + jnp.arange(taps, dtype=jnp.int32)[:, None]
    wanted = jnp.concatenate(
        [jnp.full((PAD - 1,), -1, jnp.int32), (me * frame_count - 1)[None], wanted.reshape(-1)]
    )
    holder = jnp.maximum(wanted, 0) // frame_count
    slot = jnp.zeros_like(wanted)
    for i, offset in enumerate(offsets):
        slot = jnp.where((holder ^ me) == offset, i, slot)
    line = jnp.where(wanted >= 0, slot * frame_count + wanted % frame_count, -1)[:, None]
    phases = codes.reshape(row_count, STRIDE, books).transpose(1, 0, 2)

    gain = norm_gain[None, :]
    early, middle = row_count // 4, row_count * 9 // 16
    cuts = [(middle, row_count - middle), (0, early), (early, middle - early)]
    parts = []
    for i, cut in enumerate(cuts):
        windows = (all_lines, line) if i == 1 else None
        source = held if i == 2 else (tables, conv_weight)
        part, *held = embed_conv(phases, *source, cut, windows, i < 2, i == 1)
        parts.append([part] + [swapped(part, "head", d) for d in range(1, heads_axis)])

    query = project([(parts[1], early, mine)], gain, [query_weight], "queries")
    queries, offsets = gathered(query, "tm", stages)
    weights = [key_weight, value_weight]
    groups = [(part, 0, cut[1]) for part, cut in zip(parts, cuts)]
    own = [project(some, gain, weights, "keys_values") for some in (groups[:2], groups[2:])]
    others = [swapped(some, "tm", 1) for some in own]

    owners = shards // 2
    owner_of = (me // 2) ^ jnp.asarray([offset // 2 for offset in offsets], jnp.int32)
    starts = jnp.asarray([cut[0] for cut in cuts], jnp.int32)
    place = jnp.concatenate([me * row_count + starts, (me ^ 1) * row_count + starts])
    by_core = latent_pos.reshape(owners, 2, mine)
    latent_rows = lax.dynamic_index_in_dim(by_core, me % 2, 1, False).reshape(owners * mine, 1)
    runs = [cut[1] for cut in cuts] * 2
    partials = attend(place, owner_of, queries, own + others, runs, latent_rows)
    same_core = [[2 * i + core for i in range(owners)] for core in range(2)]
    partials = lax.all_to_all(
        partials, "tm", 0, 0, axis_index_groups=same_core, tiled=True
    )
    return merge(partials, owners)


def solution(mesh):
    placed = (
        P("tm", None),
        P(None, None, "head"),
        P(None, "head", None),
        P(),
        P(None, "head"),
        P(None, "head"),
        P(None, "head"),
        P(),
    )
    return jax.shard_map(
        on_device, mesh=mesh, in_specs=placed, out_specs=P("tm", "head"), check_vma=False
    )
```
